32 devices in a mesh: dp: 4 (over y, core), fsdp: 8 (over z, x).
Axes of the slice: x: 2, y: 2, z: 4, core: 2. Of those that a mesh axis runs over, the one named last changes fastest.
Arguments:
- block_input: bfloat16 [2, 16384, 1024], P(None, ('dp', 'fsdp'))
- cotangent: bfloat16 [2, 16384, 1024], P(None, ('dp', 'fsdp')), may hold values from -6 to 6
- query_weight: bfloat16 [1024, 1024], P(('dp', 'fsdp')), may hold values from -0.1875 to 0.1875
- key_weight: bfloat16 [1024, 1024], P(('dp', 'fsdp')), may hold values from -0.1875 to 0.1875
- value_weight: bfloat16 [1024, 1024], P(('dp', 'fsdp')), may hold values from -0.1875 to 0.1875
- gate_weight: bfloat16 [1024, 1024], P(('dp', 'fsdp')), may hold values from -0.1875 to 0.1875
- out_weight: bfloat16 [1024, 1024], P(('dp', 'fsdp')), may hold values from -0.1875 to 0.1875
- first_glu: bfloat16 [1024, 2816], P(('dp', 'fsdp')), may hold values from -0.1875 to 0.1875
- second_glu: bfloat16 [1024, 2816], P(('dp', 'fsdp')), may hold values from -0.1875 to 0.1875
- down_weight: bfloat16 [2816, 1024], P(('dp', 'fsdp')), may hold values from -0.109375 to 0.109375
- seq_lengths: int32 [2, 32, 4], P(None, ('dp', 'fsdp')), may hold values from 1 to 384, 512 in all within a row
- slot_index: int32 [2, 16384], P(None, ('dp', 'fsdp')), may hold values from 0 to 4095, as said below
Outputs:
- block_output: bfloat16 [2, 16384, 1024], P(None, ('dp', 'fsdp'))
- input_grad: bfloat16 [2, 16384, 1024], P(None, ('dp', 'fsdp'))
- query_grad: float32 [1024, 1024], P(('dp', 'fsdp'))
- key_grad: float32 [1024, 1024], P(('dp', 'fsdp'))
- value_grad: float32 [1024, 1024], P(('dp', 'fsdp'))
- gate_grad: float32 [1024, 1024], P(('dp', 'fsdp'))
- out_grad: float32 [1024, 1024], P(('dp', 'fsdp'))
- first_grad: float32 [1024, 2816], P(('dp', 'fsdp'))
- second_grad: float32 [1024, 2816], P(('dp', 'fsdp'))
- down_grad: float32 [2816, 1024], P(('dp', 'fsdp'))
- stream_rms: float32 [3], replicated
The draws below stay inside these ranges and needn't reach their ends.
Inputs may be any that keep to these rules, and one draw needn't show every extreme that they name: `slot_index`: within each micro-batch and each aligned block of 4096 rows along the token dimension, the entries are a permutation of the group's slots; the 512 rows of one device name exactly 64 slots in each block of the group.
All inputs are finite; a program needn't handle non-finite values.
Results may differ from the reference program's by a relative error of at most 0.014.
Values may be sent and summed in bfloat16 or wider, within the bound.
A program may use at most 256 MiB of HBM per device.

```python
import math
import jax
import jax.numpy as jnp
import numpy as np
from jax import lax

D = 1024
HEADS = 8
HEAD_DIM = 128
FF = 2816
SLOTS = 512
MB = 2
NSEG = 4
LMAX = 384
BLOCKS = 32
GROUP = 4096
TOKENS = 16384


def draw_block_input(key, part):
    row_frac = jnp.arange(TOKENS, dtype=jnp.float32) / (TOKENS - 1)
    base = jax.random.normal(key, (MB, TOKENS, D), jnp.float32)
    scale = jnp.exp(math.log(3.0) * row_frac)
    return (base * scale[None, :, None]).astype(jnp.bfloat16)


def draw_slot_index(key, part):
    group_devices = GROUP // SLOTS
    group_count = TOKENS // GROUP
    per_pair = SLOTS // group_devices

    def one_group(group_key):
        dst_key, src_key = jax.random.split(group_key)
        dst_perm = jax.vmap(lambda sub_key: jax.random.permutation(sub_key, SLOTS))(jax.random.split(dst_key, group_devices))
        src_perm = jax.vmap(lambda sub_key: jax.random.permutation(sub_key, SLOTS))(jax.random.split(src_key, group_devices))
        src_index = jnp.arange(group_devices, dtype=jnp.int32)[:, None, None]
        dst_index = jnp.arange(group_devices, dtype=jnp.int32)[None, :, None]
        pick_rank = jnp.arange(per_pair, dtype=jnp.int32)[None, None, :]
        src_rows = src_perm[src_index, dst_index * per_pair + pick_rank]
        targets = dst_index * SLOTS + dst_perm[dst_index, pick_rank * group_devices + src_index]
        src_full = jnp.broadcast_to(src_index, src_rows.shape)
        chosen = jnp.zeros((group_devices, SLOTS), jnp.int32).at[src_full, src_rows].set(targets.astype(jnp.int32))
        return chosen.reshape(GROUP)
    all_keys = jax.random.split(key, MB * group_count)
    return jax.vmap(one_group)(all_keys).reshape(MB, TOKENS)


def levels(key, extent, cuts, least, largest):
    def one(dim, parts):
        draws = jax.random.uniform(jax.random.fold_in(jax.random.fold_in(key, 6), dim), (parts,), jnp.float32, least / len(cuts), largest / len(cuts))
        return jnp.repeat(jnp.exp(draws), extent[dim] // parts).reshape((-1,) + (1,) * (len(extent) - dim - 1))

    loudness = one(*cuts[0])
    for cut in cuts[1:]:
        loudness = loudness * one(*cut)
    return loudness


def length_profile(amount, total, limit, skew):
    loads = [(1 << 20) // math.isqrt(standing ** skew) + 1 for standing in range(2, amount + 1)]
    surplus, given = total - limit - (amount - 1), [1] * (amount - 1)
    while surplus > 0:
        movable = [i for i in range(amount - 1) if given[i] < limit]
        mass, budget = sum([loads[i] for i in movable]), surplus
        for i in movable:
            addition = min(limit - given[i], max(1, budget * loads[i] // mass), surplus)
            given[i] = given[i] + addition
            surplus = surplus - addition
    return np.array([limit] + given)


def uneven(rng, amount, total, reach, lean):
    if amount == 2:
        one = jax.random.randint(rng, (), max(1, total - reach), min(reach, total - 1) + 1)
        return jnp.stack([one, total - one])
    tallies = jnp.asarray(length_profile(amount, total, reach, lean), jnp.int32)
    couples = (amount - 1) // 2
    donor, receiver = tallies[1:1 + 2 * couples:2], tallies[2:2 + 2 * couples:2]
    slack = jnp.minimum(donor - 1, reach - receiver)
    passed = jax.random.randint(jax.random.fold_in(rng, 1), (couples,), 0, 1 << 20) % (slack + 1)
    tallies = tallies.at[1:1 + 2 * couples:2].set(donor - passed).at[2:2 + 2 * couples:2].set(receiver + passed)
    return tallies[jax.random.permutation(jax.random.fold_in(rng, 2), amount)]


def centred(key, shape, scale, reach, cuts=(), kind=jnp.bfloat16):
    drawn = jax.random.normal(key, shape, jnp.float32) * scale
    if len(cuts) > 0:
        drawn = levels(key, shape, cuts, -0.22, 0.18) * drawn
    return jnp.clip(drawn, min=-reach, max=reach).astype(kind)


def setup_inputs(seed: int = 0) -> dict:
    key_of = jax.random.split(jax.random.key(seed), 13)
    return {
        "block_input": draw_block_input(jax.random.fold_in(key_of[12], 71), 0),
        "cotangent": centred(key_of[1], (MB, TOKENS, D), 1.0, 6.0, ((1, 32),)),
        "query_weight": centred(key_of[2], (D, D), D ** -0.5, 0.1875, ((0, 32),)),
        "key_weight": centred(key_of[3], (D, D), D ** -0.5, 0.1875, ((0, 32),)),
        "value_weight": centred(key_of[4], (D, D), D ** -0.5, 0.1875, ((0, 32),)),
        "gate_weight": centred(key_of[5], (D, D), D ** -0.5, 0.1875, ((0, 32),)),
        "out_weight": centred(key_of[6], (D, D), D ** -0.5, 0.1875, ((0, 32),)),
        "first_glu": centred(key_of[7], (D, FF), D ** -0.5, 0.1875, ((0, 32),)),
        "second_glu": centred(key_of[8], (D, FF), D ** -0.5, 0.1875, ((0, 32),)),
        "down_weight": centred(key_of[9], (FF, D), FF ** -0.5, 0.109375, ((0, 32),)),
        "seq_lengths": jax.vmap(lambda own: uneven(own, NSEG, SLOTS, LMAX, 2))(jax.random.split(key_of[10], MB * BLOCKS)).reshape((MB, BLOCKS, NSEG)).astype(jnp.int32),
        "slot_index": draw_slot_index(jax.random.fold_in(key_of[12], 71), 0),
    }


EPS = 1e-06
HIGH = lax.Precision.HIGHEST

@jax.custom_vjp
def low(v):
    return lax.optimization_barrier(v.astype(jnp.bfloat16)).astype(jnp.float32)

@jax.custom_vjp
def low_back(v):
    return v

def low_keep(v):
    return (low(v), None)

def low_pass(kept, grad):
    return (grad,)

def back_keep(v):
    return (v, None)

def back_low(kept, grad):
    return (low(grad),)
low.defvjp(low_keep, low_pass)
low_back.defvjp(back_keep, back_low)

def rms_norm(vector):
    return vector * lax.rsqrt(lax.optimization_barrier(jnp.mean(vector * vector, axis=-1, keepdims=True)) + EPS)

def swish_act(vector):
    return vector * jax.nn.sigmoid(vector)

def block_frame(block_lengths):
    seg_ends = jnp.cumsum(block_lengths)
    starts = seg_ends - block_lengths
    places = jnp.arange(SLOTS, dtype=jnp.int32)
    member = (places[:, None] >= starts[None, :]) & (places[:, None] < seg_ends[None, :])
    segment = lax.optimization_barrier(jnp.sum(jnp.where(member, jnp.arange(NSEG, dtype=jnp.int32)[None, :], 0), axis=1))
    offset = lax.optimization_barrier(jnp.sum(jnp.where(member, starts[None, :], 0), axis=1))
    position = places - offset
    valid_rows = (places < seg_ends[NSEG - 2]).astype(jnp.float32)
    distance = places[:, None] - places[None, :]
    linked = (segment[:, None] == segment[None, :]) & (distance >= 0)
    head_ids = jnp.arange(HEADS, dtype=jnp.float32)
    log_decay = -jnp.exp2(-(head_ids + 1.0) * 8.0 / HEADS)
    steps_back = jnp.maximum(distance, 0).astype(jnp.float32)
    decay_mat = jnp.where(linked[None], jnp.exp(log_decay[:, None, None] * steps_back[None]), 0.0)
    frequency = jnp.exp(-math.log(10000.0) * jnp.arange(HEAD_DIM, dtype=jnp.float32) / HEAD_DIM)
    angles = position.astype(jnp.float32)[:, None] * frequency[None, :]
    return (jnp.cos(angles), jnp.sin(angles), decay_mat, valid_rows)

def rotate(vector, cosine, sine_vals):
    return jnp.concatenate([vector * cosine[:, None, :], vector * sine_vals[:, None, :]], axis=-1)

def layer(block_rows, matrices, cosine, sine_vals, decay_mat, valid_rows):
    query_mat, key_mat, value_mat, gate_mat, out_mat, first_mat, second_mat, down_mat = matrices
    row_count = block_rows.shape[0]
    normed_in = low(rms_norm(block_rows))
    query_pre = low_back(jnp.dot(normed_in, query_mat, precision=HIGH))
    key_pre = low_back(jnp.dot(normed_in, key_mat, precision=HIGH))
    value_pre = low_back(jnp.dot(normed_in, value_mat, precision=HIGH))
    gate_pre = low_back(jnp.dot(normed_in, gate_mat, precision=HIGH))
    query_rot = low(rotate(swish_act(query_pre).reshape(row_count, HEADS, HEAD_DIM), cosine, sine_vals))
    key_rot = low(rotate(swish_act(key_pre).reshape(row_count, HEADS, HEAD_DIM), cosine, sine_vals))
    value_heads = low(value_pre).reshape(row_count, HEADS, HEAD_DIM)
    scores = low_back(jnp.einsum('thc,shc->hts', query_rot, key_rot, precision=HIGH))
    probs = low(scores * decay_mat)
    mixed = low_back(jnp.einsum('hts,shc->thc', probs, value_heads, precision=HIGH).reshape(row_count, HEADS * HEAD_DIM))
    gated = low(rms_norm(mixed) * gate_pre)
    attn_out = low_back(jnp.dot(gated, out_mat, precision=HIGH))
    stream = block_rows + attn_out
    normed_mid = low(rms_norm(stream))
    first = low_back(jnp.dot(normed_mid, first_mat, precision=HIGH))
    second = low_back(jnp.dot(normed_mid, second_mat, precision=HIGH))
    product = low(first * second)
    glu_out = low_back(jnp.dot(product, down_mat, precision=HIGH))
    result = (stream + glu_out) * valid_rows[:, None]
    square_sums = jnp.stack([jnp.sum(result * result), jnp.sum(attn_out * attn_out * valid_rows[:, None]), jnp.sum(glu_out * glu_out * valid_rows[:, None])])
    return (result, square_sums)

def reference(block_input, cotangent, query_weight, key_weight, value_weight, gate_weight, out_weight, first_glu, second_glu, down_weight, seq_lengths, slot_index):
    matrices = tuple((mat.astype(jnp.float32) for mat in (query_weight, key_weight, value_weight, gate_weight, out_weight, first_glu, second_glu, down_weight)))
    block_total = TOKENS // SLOTS
    group_base = jnp.arange(TOKENS, dtype=jnp.int32) // GROUP * GROUP

    def micro_step(carry_in, micro_item):
        rows_given, grads_given, lengths_given, slots_given = micro_item
        slot_of = group_base + slots_given.astype(jnp.int32)
        rows_slot = jnp.zeros((TOKENS, D), jnp.float32).at[slot_of].set(rows_given.astype(jnp.float32)).reshape(block_total, SLOTS, D)
        grads_slot = jnp.zeros((TOKENS, D), jnp.float32).at[slot_of].set(grads_given.astype(jnp.float32)).reshape(block_total, SLOTS, D)

        def block_step(carry_blk, block_item):
            block_rows, block_grad, block_lengths = block_item
            cosine, sine_vals, decay_mat, valid_rows = block_frame(block_lengths)

            def layer_fn(row_input, mats_in):
                return layer(row_input, mats_in, cosine, sine_vals, decay_mat, valid_rows)
            results, back_fn, square_sums = jax.vjp(layer_fn, block_rows, matrices, has_aux=True)
            row_grads, mat_grads = back_fn(block_grad)
            gradients, stat_sums, valid_count = carry_blk
            gradients = tuple((total + piece for total, piece in zip(gradients, mat_grads)))
            return ((gradients, stat_sums + square_sums, valid_count + jnp.sum(valid_rows)), (results, row_grads))
        carry_out, (results, row_grads) = lax.scan(block_step, carry_in, (rows_slot, grads_slot, lengths_given))
        out_given = results.reshape(TOKENS, D)[slot_of]
        grad_given = row_grads.reshape(TOKENS, D)[slot_of]
        return (carry_out, (out_given.astype(jnp.bfloat16), grad_given.astype(jnp.bfloat16)))
    start = (tuple((jnp.zeros(mat.shape, jnp.float32) for mat in matrices)), jnp.zeros((3,), jnp.float32), jnp.zeros((), jnp.float32))
    (gradients, stat_sums, valid_count), (outputs, input_grads) = lax.scan(micro_step, start, (block_input, cotangent, seq_lengths, slot_index))
    stream_rms = jnp.sqrt(stat_sums / (valid_count * D))
    return (outputs, input_grads, gradients[0], gradients[1], gradients[2], gradients[3], gradients[4], gradients[5], gradients[6], gradients[7], stream_rms)
```

```python
import math

import jax
import jax.numpy as jnp
from jax import lax
from jax.sharding import PartitionSpec as P

HEADS = 8
HEAD_DIM = 128
NSEG = 4


EPS = 1e-06


def rms_norm(vector):
    return vector * lax.rsqrt(jnp.mean(vector * vector, axis=-1, keepdims=True) + EPS)


def norm_back(vector, grad_in):
    inv_rms = lax.rsqrt(jnp.mean(vector * vector, axis=-1, keepdims=True) + EPS)
    unit_rows = vector * inv_rms
    return inv_rms * (grad_in - unit_rows * jnp.mean(grad_in * unit_rows, axis=-1, keepdims=True))


def swish_act(vector):
    return vector * jax.nn.sigmoid(vector)


def swish_slope(vector):
    sigmoid_val = jax.nn.sigmoid(vector)
    return sigmoid_val + vector * sigmoid_val * (1.0 - sigmoid_val)


def against(grad_rows, matrix):
    return lax.dot_general(
        grad_rows, matrix, (((1,), (1,)), ((), ())), preferred_element_type=jnp.float32
    )


def outer_sum(left, right):
    return lax.dot_general(
        left, right, (((0,), (0,)), ((), ())), preferred_element_type=jnp.float32
    )


def matmul(left, right):
    return jnp.dot(left, right, preferred_element_type=jnp.float32)


def block_frame(block_lengths, slot_count):
    seg_ends = jnp.cumsum(block_lengths)
    starts = seg_ends - block_lengths
    places = jnp.arange(slot_count, dtype=jnp.int32)
    member = (places[:, None] >= starts[None, :]) & (places[:, None] < seg_ends[None, :])
    segment = jnp.sum(jnp.where(member, jnp.arange(NSEG, dtype=jnp.int32)[None, :], 0), axis=1)
    offset = jnp.sum(jnp.where(member, starts[None, :], 0), axis=1)
    position = places - offset
    valid_rows = (places < seg_ends[NSEG - 2]).astype(jnp.float32)
    distance = places[:, None] - places[None, :]
    linked = (segment[:, None] == segment[None, :]) & (distance >= 0)
    head_ids = jnp.arange(HEADS, dtype=jnp.float32)
    log_decay = -jnp.exp2(-(head_ids + 1.0) * 8.0 / HEADS)
    steps_back = jnp.maximum(distance, 0).astype(jnp.float32)
    decay_mat = jnp.where(linked[None], jnp.exp(log_decay[:, None, None] * steps_back[None]), 0.0)
    frequency = jnp.exp(-math.log(10000.0) * jnp.arange(HEAD_DIM, dtype=jnp.float32) / HEAD_DIM)
    angles = position.astype(jnp.float32)[:, None] * frequency[None, :]
    return (jnp.cos(angles), jnp.sin(angles), decay_mat, valid_rows)


def rotate(vector, cosine, sine_vals):
    return jnp.concatenate([vector * cosine[:, None, :], vector * sine_vals[:, None, :]], axis=-1)


def unrotate(grad_rot, cosine, sine_vals, pre_act):
    row_count = grad_rot.shape[0]
    folded = (
        grad_rot[..., :HEAD_DIM] * cosine[:, None, :]
        + grad_rot[..., HEAD_DIM:] * sine_vals[:, None, :]
    )
    return (folded.reshape(row_count, HEADS * HEAD_DIM) * swish_slope(pre_act)).astype(jnp.bfloat16)


def sort_slots(slots, slot_count):
    rank = jnp.sum((slots[:, None, :] < slots[:, :, None]).astype(jnp.int32), axis=2)
    places = jnp.arange(slot_count, dtype=jnp.int32)
    hit = rank[:, None, :] == places[None, :, None]
    ordered = jnp.sum(jnp.where(hit, slots[:, None, :], 0), axis=2)
    return hit.astype(jnp.bfloat16), ordered


def pick(selector, rows):
    return jnp.einsum("mrs,msd->mrd", selector, rows, preferred_element_type=jnp.float32)


def put_back(selector, rows):
    return jnp.einsum("mrs,mrd->msd", selector, rows, preferred_element_type=jnp.float32)


def swap_rows(rows, peer_count):
    micro_count, slot_count, width = rows.shape
    split = rows.reshape(micro_count, peer_count, slot_count // peer_count, width)
    moved = lax.all_to_all(split, "fsdp", split_axis=1, concat_axis=1, tiled=True)
    return moved.reshape(micro_count, slot_count, width)


def gather_rows(shard):
    return lax.all_gather(shard, ("dp", "fsdp"), axis=0, tiled=True)


def scatter_sum(total):
    return lax.psum_scatter(total, ("dp", "fsdp"), scatter_dimension=0, tiled=True)


def body(
    block_input,
    cotangent,
    query_weight,
    key_weight,
    value_weight,
    gate_weight,
    out_weight,
    first_glu,
    second_glu,
    down_weight,
    seq_lengths,
    slot_index,
):
    peer_count = lax.axis_size("fsdp")
    micro_count, slot_count, width = block_input.shape
    ff_width = first_glu.shape[1]
    row_count = micro_count * slot_count

    front_mat = gather_rows(
        jnp.concatenate([query_weight, key_weight, value_weight, gate_weight], axis=1)
    )
    out_mat = gather_rows(out_weight)
    glu_mat = gather_rows(jnp.concatenate([first_glu, second_glu], axis=1))
    down_mat = gather_rows(down_weight)

    send_hit, ordered = sort_slots(slot_index, slot_count)
    landing = swap_rows((ordered % slot_count)[:, :, None], peer_count)[:, :, 0]
    both = jnp.concatenate([block_input, cotangent], axis=2)
    sent = pick(send_hit, both).astype(jnp.bfloat16)
    got = swap_rows(sent, peer_count)
    places = jnp.arange(slot_count, dtype=jnp.int32)
    land_hit = (landing[:, :, None] == places[None, None, :]).astype(jnp.bfloat16)
    slot_rows = put_back(land_hit, got)
    stream_in = slot_rows[:, :, :width].reshape(row_count, width)
    grad_in = slot_rows[:, :, width:].reshape(row_count, width)

    cosine, sine_vals, decay_mat, valid_rows = jax.vmap(
        lambda lengths: block_frame(lengths, slot_count)
    )(seq_lengths[:, 0])
    valid_rows = valid_rows.reshape(row_count)
    cosine = cosine.reshape(row_count, HEAD_DIM)
    sine_vals = sine_vals.reshape(row_count, HEAD_DIM)

    def heads(array):
        return array.reshape(micro_count, slot_count, HEADS, -1)

    normed_in = rms_norm(stream_in).astype(jnp.bfloat16)
    front = matmul(normed_in, front_mat)
    query_pre, key_pre, value_pre, gate_pre = (
        front[:, i * width : (i + 1) * width] for i in range(4)
    )
    query_rot = heads(
        rotate(swish_act(query_pre).reshape(row_count, HEADS, HEAD_DIM), cosine, sine_vals).astype(
            jnp.bfloat16
        )
    )
    key_rot = heads(
        rotate(swish_act(key_pre).reshape(row_count, HEADS, HEAD_DIM), cosine, sine_vals).astype(
            jnp.bfloat16
        )
    )
    value_heads = heads(value_pre.astype(jnp.bfloat16))
    scores = jnp.einsum("mthc,mshc->mhts", query_rot, key_rot, preferred_element_type=jnp.float32)
    probs = (scores * decay_mat).astype(jnp.bfloat16)
    mixed = jnp.einsum(
        "mhts,mshc->mthc", probs, value_heads, preferred_element_type=jnp.float32
    ).reshape(row_count, width)
    mixed_unit = rms_norm(mixed)
    gated = (mixed_unit * gate_pre).astype(jnp.bfloat16)
    attn_out = matmul(gated, out_mat)
    stream = stream_in + attn_out
    normed_mid = rms_norm(stream).astype(jnp.bfloat16)
    glu_in = matmul(normed_mid, glu_mat)
    first, second = glu_in[:, :ff_width], glu_in[:, ff_width:]
    product = (first * second).astype(jnp.bfloat16)
    glu_out = matmul(product, down_mat)
    result = (stream + glu_out) * valid_rows[:, None]
    square_sums = jnp.stack(
        [
            jnp.sum(result * result),
            jnp.sum(attn_out * attn_out * valid_rows[:, None]),
            jnp.sum(glu_out * glu_out * valid_rows[:, None]),
        ]
    )
    result_rows = result.astype(jnp.bfloat16)

    grad_out = grad_in * valid_rows[:, None]
    grad_glu = grad_out.astype(jnp.bfloat16)
    down_part = outer_sum(product, grad_glu).astype(jnp.bfloat16)
    grad_product = against(grad_glu, down_mat)
    grad_pair = jnp.concatenate(
        [
            (grad_product * second).astype(jnp.bfloat16),
            (grad_product * first).astype(jnp.bfloat16),
        ],
        axis=1,
    )
    glu_part = outer_sum(normed_mid, grad_pair).astype(jnp.bfloat16)
    grad_stream = grad_out + norm_back(stream, against(grad_pair, glu_mat))
    grad_attn = grad_stream.astype(jnp.bfloat16)
    out_part = outer_sum(gated, grad_attn).astype(jnp.bfloat16)
    grad_gated = against(grad_attn, out_mat)
    grad_gate = (grad_gated * mixed_unit).astype(jnp.bfloat16)
    grad_mixed = heads(norm_back(mixed, grad_gated * gate_pre).astype(jnp.bfloat16))
    grad_value = (
        jnp.einsum("mhts,mthc->mshc", probs, grad_mixed, preferred_element_type=jnp.float32)
        .astype(jnp.bfloat16)
        .reshape(row_count, width)
    )
    grad_probs = jnp.einsum(
        "mthc,mshc->mhts", grad_mixed, value_heads, preferred_element_type=jnp.float32
    )
    grad_scores = (grad_probs * decay_mat).astype(jnp.bfloat16)
    grad_qrot = jnp.einsum(
        "mhts,mshc->mthc", grad_scores, key_rot, preferred_element_type=jnp.float32
    ).reshape(row_count, HEADS, 2 * HEAD_DIM)
    grad_krot = jnp.einsum(
        "mhts,mthc->mshc", grad_scores, query_rot, preferred_element_type=jnp.float32
    ).reshape(row_count, HEADS, 2 * HEAD_DIM)
    grad_query = unrotate(grad_qrot, cosine, sine_vals, query_pre)
    grad_key = unrotate(grad_krot, cosine, sine_vals, key_pre)
    grad_front = jnp.concatenate([grad_query, grad_key, grad_value, grad_gate], axis=1)
    front_part = outer_sum(normed_in, grad_front).astype(jnp.bfloat16)
    grad_rows = grad_stream + norm_back(stream_in, against(grad_front, front_mat))

    replies = jnp.concatenate([result_rows, grad_rows.astype(jnp.bfloat16)], axis=1)
    replies = replies.reshape(micro_count, slot_count, 2 * width)
    back = swap_rows(pick(land_hit, replies).astype(jnp.bfloat16), peer_count)
    given = put_back(send_hit, back).astype(jnp.bfloat16)

    down_grad = scatter_sum(down_part).astype(jnp.float32)
    glu_grad = scatter_sum(glu_part).astype(jnp.float32)
    out_grad = scatter_sum(out_part).astype(jnp.float32)
    front_grad = scatter_sum(front_part).astype(jnp.float32)
    total_sums, total_count = lax.psum((square_sums, jnp.sum(valid_rows)), ("dp", "fsdp"))
    stream_rms = jnp.sqrt(total_sums / (total_count * width))
    return (
        given[:, :, :width],
        given[:, :, width:],
        front_grad[:, :width],
        front_grad[:, width : 2 * width],
        front_grad[:, 2 * width : 3 * width],
        front_grad[:, 3 * width :],
        out_grad,
        glu_grad[:, :ff_width],
        glu_grad[:, ff_width:],
        down_grad,
        stream_rms,
    )


def solution(mesh):
    in_specs = (
        P(None, ("dp", "fsdp"), None),
        P(None, ("dp", "fsdp"), None),
        P(("dp", "fsdp"), None),
        P(("dp", "fsdp"), None),
        P(("dp", "fsdp"), None),
        P(("dp", "fsdp"), None),
        P(("dp", "fsdp"), None),
        P(("dp", "fsdp"), None),
        P(("dp", "fsdp"), None),
        P(("dp", "fsdp"), None),
        P(None, ("dp", "fsdp"), None),
        P(None, ("dp", "fsdp")),
    )
    out_specs = (
        P(None, ("dp", "fsdp"), None),
        P(None, ("dp", "fsdp"), None),
        P(("dp", "fsdp"), None),
        P(("dp", "fsdp"), None),
        P(("dp", "fsdp"), None),
        P(("dp", "fsdp"), None),
        P(("dp", "fsdp"), None),
        P(("dp", "fsdp"), None),
        P(("dp", "fsdp"), None),
        P(("dp", "fsdp"), None),
        P(),
    )
    return jax.shard_map(body, mesh=mesh, in_specs=in_specs, out_specs=out_specs, check_vma=False)
```
